32 devices in a mesh: shot: 8 (over z, y), rcv: 4 (over x, core).
Axes of the slice: x: 2, y: 2, z: 4, core: 2. Of those that a mesh axis runs over, the one named last changes fastest.
Arguments:
- data_matrix: bfloat16 [2, 16, 1024, 1024], P(None, None, 'shot', 'rcv'), may hold values from -12 to 12
- shot_records: bfloat16 [2, 16, 1024, 1024], P(None, None, 'rcv', 'shot'), may hold values from -4 to 4
- live: int32 [1024, 1024], P('rcv', 'shot'), may hold values 0 or 1
Outputs:
- predicted: bfloat16 [2, 16, 1024, 1024], P(None, None, 'rcv', 'shot')
- primaries: bfloat16 [2, 16, 1024, 1024], P(None, None, 'rcv', 'shot')
The draws below stay inside these ranges and needn't reach their ends.
All inputs are finite; a program needn't handle non-finite values. No bound on the sum of `live` on one device may be relied on, other than what follows from the above.
Results may differ from the reference program's by a relative error of at most 0.013.
Values may be sent and summed in bfloat16 or wider, within the bound.
A program may use at most 128 MiB of HBM per device.

```python
import math
import jax
import jax.numpy as jnp
from jax import lax

NPTS = 1024
F_WIN = 16
SHOTS = 1024
N_RCV = 4


def draw_data_matrix(key, part):
    first, second, third = jax.random.split(key, 3)
    shape = (2, F_WIN, NPTS, NPTS)
    noise = jnp.clip(jax.random.normal(first, shape, jnp.float32), -4.0, 4.0)
    place = jnp.arange(NPTS, dtype=jnp.float32) / (NPTS - 1)
    rough = jax.random.uniform(second, (NPTS,), jnp.float32, -0.5, 0.5)
    scale = jnp.exp(math.log(3.0) * place + math.log(10.0) * rough)
    gain = jax.random.uniform(third, (2, F_WIN, NPTS), jnp.float32, 0.5, 1.0)
    rows = jnp.arange(NPTS)
    eye = (rows[:, None] == rows[None, :]).astype(jnp.float32)
    values = (gain[..., None] * eye + 0.5 * noise / math.sqrt(NPTS)) * scale[:, None]
    return values.astype(jnp.bfloat16)


def draw_shot_records(key, part):
    first, second = jax.random.split(key, 2)
    shape = (2, F_WIN, NPTS, SHOTS)
    noise = jnp.clip(jax.random.normal(first, shape, jnp.float32), -4.0, 4.0)
    scale = 0.1 * jnp.exp(math.log(10.0) * jax.random.uniform(second, (SHOTS,), jnp.float32, 0.0, 1.0))
    return (noise * scale).astype(jnp.bfloat16)


def place_ends(values, rng, smallest, top_value):
    spot = [jax.random.randint(jax.random.fold_in(rng, axis), (), 0, length) for axis, length in enumerate(values.shape)]
    main_axis = values.shape.index(max(values.shape))
    next_to = spot[:main_axis] + [(spot[main_axis] + 1) % values.shape[main_axis]] + spot[main_axis + 1:]
    return values.at[tuple(spot)].set(smallest).at[tuple(next_to)].set(top_value)


def setup_inputs(seed: int = 0) -> dict:
    streams_of = jax.random.split(jax.random.key(seed), 4)
    return {
        "data_matrix": draw_data_matrix(jax.random.fold_in(streams_of[3], 71), 0),
        "shot_records": draw_shot_records(jax.random.fold_in(streams_of[3], 71), 0),
        "live": place_ends((jax.random.randint(streams_of[2], (NPTS, SHOTS), 0, 8) < 7).astype(jnp.int32), jax.random.fold_in(streams_of[2], 1), 0, 1),
    }


def one_slice(inputs):
    matrix, records = inputs
    group = NPTS // N_RCV
    total = jnp.zeros((2, NPTS, records.shape[2]), jnp.float32)
    for index in range(N_RCV):
        left = matrix[:, :, index * group:(index + 1) * group].astype(jnp.float32)
        right = records[:, index * group:(index + 1) * group, :].astype(jnp.float32)
        prod = jnp.einsum("ark,bks->abrs", left, right)
        term = jnp.stack((prod[0, 0] - prod[1, 1], prod[0, 1] + prod[1, 0])).astype(jnp.bfloat16)
        term = lax.optimization_barrier(term)
        total = total + term.astype(jnp.float32)
    return total


def reference(data_matrix, shot_records, live):
    records = shot_records * live.astype(jnp.bfloat16)[None, None]
    slices = lax.map(one_slice, (jnp.moveaxis(data_matrix, 1, 0), jnp.moveaxis(records, 1, 0)))
    total = jnp.moveaxis(slices, 0, 1)
    rec = records.astype(jnp.float32)
    num_re = jnp.mean(total[0] * rec[0] + total[1] * rec[1], axis=1)
    num_im = jnp.mean(total[0] * rec[1] - total[1] * rec[0], axis=1)
    power = jnp.mean(total[0] * total[0] + total[1] * total[1], axis=1) + 1e-6
    filt_re = (num_re / power)[:, None, :]
    filt_im = (num_im / power)[:, None, :]
    out_re = rec[0] - (filt_re * total[0] - filt_im * total[1])
    out_im = rec[1] - (filt_re * total[1] + filt_im * total[0])
    primaries = jnp.stack((out_re, out_im)).astype(jnp.bfloat16)
    return total.astype(jnp.bfloat16), primaries
```

```python
import functools

import jax
import jax.numpy as jnp
from jax import lax
from jax.experimental import pallas as pl
from jax.experimental.pallas import tpu as pltpu
from jax.sharding import PartitionSpec as P

MESH = pl.DeviceIdType.MESH


def each(start, stop, body):
    def step(index, carry):
        body(index)
        return carry

    lax.fori_loop(start, stop, step, 0)


def exchange_kernel(
    n_shot, n_rcv,
    d_ref, s_ref, live_ref, o_ref, filt_ref,
    dbuf, pbuf, srec, live_v, rec, mbuf, fbuf,
    load_sem, d_send, d_recv, p_send, p_recv, o_send, o_recv, f_send, f_recv,
):
    n_freq, own_rows = d_ref.shape[1], d_ref.shape[2]
    own_pts, own_shots = s_ref.shape[2], s_ref.shape[3]
    points = own_pts * n_rcv
    per_group = n_freq // n_rcv
    n_groups = n_shot // per_group
    me_i, me_j = lax.axis_index("shot"), lax.axis_index("rcv")
    group, place = lax.div(me_i, per_group), lax.rem(me_i, per_group)
    my_f = place * n_rcv + me_j
    me = me_i * n_rcv + me_j
    n_dev = n_shot * n_rcv

    load_s = pltpu.make_async_copy(s_ref, srec, load_sem.at[0])
    load_live = pltpu.make_async_copy(live_ref, live_v, load_sem.at[1])
    load_s.start()
    load_live.start()

    barrier = pltpu.get_barrier_semaphore()

    def greet(k):
        other = lax.rem(me + k, n_dev)
        pl.semaphore_signal(
            barrier, inc=1, device_id=(lax.div(other, n_rcv), lax.rem(other, n_rcv)), device_id_type=MESH
        )

    each(1, n_dev, greet)
    pl.semaphore_wait(barrier, n_dev - 1)

    def home(g, f):
        return (g * per_group + lax.div(f, n_rcv), lax.rem(f, n_rcv))

    def d_dst(i, j):
        return dbuf.at[j, :, pl.ds(pl.multiple_of(i * own_rows, own_rows), own_rows), :]

    def d_copy(m):
        f = lax.rem(my_f + lax.div(m, n_groups), n_freq)
        g = lax.rem(group + lax.rem(m, n_groups), n_groups)
        return pltpu.make_async_remote_copy(
            src_ref=d_ref.at[:, f], dst_ref=d_dst(me_i, me_j), send_sem=d_send.at[m], recv_sem=d_recv.at[me],
            device_id=home(g, f), device_id_type=MESH,
        )

    def p_dst(b, j):
        return pbuf.at[b, pl.ds(pl.multiple_of(j * own_pts, own_pts), own_pts), :]

    def p_copy(k):
        f = lax.rem(my_f + k, n_freq)
        return pltpu.make_async_remote_copy(
            src_ref=rec.at[f], dst_ref=p_dst(place, me_j), send_sem=p_send.at[k], recv_sem=p_recv.at[my_f],
            device_id=home(group, f), device_id_type=MESH,
        )

    pltpu.make_async_copy(d_ref.at[:, my_f], d_dst(me_i, me_j), d_recv.at[me]).start()
    each(1, n_groups * n_freq, lambda m: d_copy(m).start())

    load_s.wait()
    load_live.wait()

    def mask(f):
        keep = live_v[...].astype(jnp.bfloat16)
        rec[f, :, :own_shots] = srec[0, f] * keep
        rec[f, :, own_shots:] = srec[1, f] * keep

    mask(my_f)
    pltpu.make_async_copy(rec.at[my_f], p_dst(place, me_j), p_recv.at[my_f]).start()

    def send_p(k):
        mask(lax.rem(my_f + k, n_freq))
        p_copy(k).start()

    each(1, n_freq, send_p)

    def p_arrived(n):
        dst = p_dst(lax.div(n, n_rcv), lax.rem(n, n_rcv))
        pltpu.make_async_copy(dst, dst, p_recv.at[n]).wait()

    def d_arrived(n):
        dst = d_dst(lax.div(n, n_rcv), lax.rem(n, n_rcv))
        pltpu.make_async_copy(dst, dst, d_recv.at[n]).wait()

    each(0, n_freq, p_arrived)
    each(0, n_dev, d_arrived)

    def turn(kb, jj):
        return lax.rem(place + kb, per_group), lax.rem(me_j + jj, n_rcv)

    def o_src(b, j):
        return mbuf.at[b, pl.ds(pl.multiple_of(j * own_pts, own_pts), own_pts), :]

    def o_copy(n):
        b, j = turn(lax.div(n, n_rcv), lax.rem(n, n_rcv))
        return pltpu.make_async_remote_copy(
            src_ref=o_src(b, j), dst_ref=o_ref.at[my_f], send_sem=o_send.at[n], recv_sem=o_recv.at[my_f],
            device_id=(group * per_group + b, j), device_id_type=MESH,
        )

    def f_copy(n):
        b, j = turn(lax.div(n, n_rcv), lax.rem(n, n_rcv))
        return pltpu.make_async_remote_copy(
            src_ref=fbuf.at[b], dst_ref=filt_ref.at[my_f], send_sem=f_send.at[n], recv_sem=f_recv.at[my_f],
            device_id=(group * per_group + b, j), device_id_type=MESH,
        )

    def shot_block(kb):
        def row_tile(jj, sums):
            b, j = turn(kb, jj)
            rows = pl.ds(pl.multiple_of(j * own_pts, own_pts), own_pts)
            left = right = None
            for h in range(n_rcv):
                block = pbuf[b, h * own_pts:(h + 1) * own_pts, :]
                one = jnp.dot(dbuf[h, 0, rows, :], block, preferred_element_type=jnp.float32)
                two = jnp.dot(dbuf[h, 1, rows, :], block, preferred_element_type=jnp.float32)
                left = one if left is None else left + one
                right = two if right is None else right + two
            m_re = left[:, :own_shots] - right[:, own_shots:]
            m_im = left[:, own_shots:] + right[:, :own_shots]
            mbuf[b, rows, :own_shots] = m_re.astype(jnp.bfloat16)
            mbuf[b, rows, own_shots:] = m_im.astype(jnp.bfloat16)
            n = kb * n_rcv + jj

            @pl.when(n == 0)
            def _():
                pltpu.make_async_copy(o_src(b, j), o_ref.at[my_f], o_recv.at[my_f]).start()

            @pl.when(n > 0)
            def _():
                o_copy(n).start()

            p_re = pbuf[b, rows, :own_shots].astype(jnp.float32)
            p_im = pbuf[b, rows, own_shots:].astype(jnp.float32)

            def down(value):
                return jnp.sum(value.reshape(own_pts // 8, 8, own_shots), axis=0)

            return (
                sums[0] + down(m_re * p_re + m_im * p_im),
                sums[1] + down(m_re * p_im - m_im * p_re),
                sums[2] + down(m_re * m_re + m_im * m_im),
            )

        zero = jnp.zeros((8, own_shots), jnp.float32)
        sums = lax.fori_loop(0, n_rcv, row_tile, (zero, zero, zero))
        num_re, num_im, power = (jnp.sum(v, axis=0, keepdims=True) / float(points) for v in sums)
        power = power + 1e-6
        row = lax.broadcasted_iota(jnp.int32, (8, own_shots), 0)
        b, _ = turn(kb, 0)
        fbuf[b] = jnp.where(row < 4, num_re / power, num_im / power)

        @pl.when(kb == 0)
        def _():
            pltpu.make_async_copy(fbuf.at[b], filt_ref.at[my_f], f_recv.at[my_f]).start()

        @pl.when(kb > 0)
        def _():
            f_copy(kb * n_rcv).start()

        each(1, n_rcv, lambda jj: f_copy(kb * n_rcv + jj).start())

    each(0, per_group, shot_block)

    def result_arrived(n):
        pltpu.make_async_copy(o_ref.at[n], o_ref.at[n], o_recv.at[n]).wait()
        pltpu.make_async_copy(filt_ref.at[n], filt_ref.at[n], f_recv.at[n]).wait()

    each(0, n_freq, result_arrived)

    each(1, n_groups * n_freq, lambda m: d_copy(m).wait_send())
    each(1, n_freq, lambda k: p_copy(k).wait_send())
    each(1, n_freq, lambda n: o_copy(n).wait_send())
    each(1, n_freq, lambda n: f_copy(n).wait_send())


def subtract_kernel(o_ref, filt_ref, s_ref, live_ref, pred_ref, prim_ref):
    shots = s_ref.shape[3]
    keep = live_ref[...].astype(jnp.bfloat16)
    for f in range(o_ref.shape[0]):
        re, im = o_ref[f, :, :shots], o_ref[f, :, shots:]
        pred_ref[0, f] = re
        pred_ref[1, f] = im
        re, im = re.astype(jnp.float32), im.astype(jnp.float32)
        filt_re, filt_im = filt_ref[f, 0:1, :], filt_ref[f, 4:5, :]
        rec_re = (s_ref[0, f] * keep).astype(jnp.float32)
        rec_im = (s_ref[1, f] * keep).astype(jnp.float32)
        prim_ref[0, f] = (rec_re - (filt_re * re - filt_im * im)).astype(jnp.bfloat16)
        prim_ref[1, f] = (rec_im - (filt_re * im + filt_im * re)).astype(jnp.bfloat16)


def shards(n_shot, n_rcv, data_matrix, shot_records, live):
    _, n_freq, own_rows, own_pts = data_matrix.shape
    own_shots = shot_records.shape[3]
    points = own_pts * n_rcv
    per_group = n_freq // n_rcv
    n_groups = n_shot // per_group
    anywhere = pl.BlockSpec(memory_space=pl.ANY)
    dma = pltpu.SemaphoreType.DMA
    multiples, filt = pl.pallas_call(
        functools.partial(exchange_kernel, n_shot, n_rcv),
        out_shape=(
            jax.ShapeDtypeStruct((n_freq, own_pts, 2 * own_shots), jnp.bfloat16),
            jax.ShapeDtypeStruct((n_freq, 8, own_shots), jnp.float32),
        ),
        in_specs=[anywhere] * 3,
        out_specs=(anywhere, anywhere),
        scratch_shapes=[
            pltpu.VMEM((n_rcv, 2, points, own_pts), jnp.bfloat16),
            pltpu.VMEM((per_group, points, 2 * own_shots), jnp.bfloat16),
            pltpu.VMEM((2, n_freq, own_pts, own_shots), jnp.bfloat16),
            pltpu.VMEM((own_pts, own_shots), jnp.int32),
            pltpu.VMEM((n_freq, own_pts, 2 * own_shots), jnp.bfloat16),
            pltpu.VMEM((per_group, points, 2 * own_shots), jnp.bfloat16),
            pltpu.VMEM((per_group, 8, own_shots), jnp.float32),
            dma((2,)),
            dma((n_groups * n_freq,)),
            dma((n_shot * n_rcv,)),
            dma((n_freq,)),
            dma((n_freq,)),
            dma((n_freq,)),
            dma((n_freq,)),
            dma((n_freq,)),
            dma((n_freq,)),
        ],
        compiler_params=pltpu.CompilerParams(
            collective_id=0, has_side_effects=True, vmem_limit_bytes=32 * 1024 * 1024
        ),
    )(data_matrix, shot_records, live)
    step = 4
    pair = pl.BlockSpec((2, step, own_pts, own_shots), lambda f: (0, f, 0, 0))
    out = jax.ShapeDtypeStruct((2, n_freq, own_pts, own_shots), jnp.bfloat16)
    return pl.pallas_call(
        subtract_kernel,
        grid=(n_freq // step,),
        out_shape=(out, out),
        in_specs=[
            pl.BlockSpec((step, own_pts, 2 * own_shots), lambda f: (f, 0, 0)),
            pl.BlockSpec((step, 8, own_shots), lambda f: (f, 0, 0)),
            pair,
            pl.BlockSpec((own_pts, own_shots), lambda f: (0, 0)),
        ],
        out_specs=(pair, pair),
        compiler_params=pltpu.CompilerParams(vmem_limit_bytes=24 * 1024 * 1024),
    )(multiples, filt, shot_records, live)


def solution(mesh):
    in_specs = (P(None, None, "shot", "rcv"), P(None, None, "rcv", "shot"), P("rcv", "shot"))
    out_specs = (P(None, None, "rcv", "shot"), P(None, None, "rcv", "shot"))
    body = functools.partial(shards, mesh.shape["shot"], mesh.shape["rcv"])
    return jax.shard_map(body, mesh=mesh, in_specs=in_specs, out_specs=out_specs, check_vma=False)
```

```python
import functools

import jax
import jax.numpy as jnp
from jax import lax
from jax.experimental import pallas as pl
from jax.experimental.pallas import tpu as pltpu
from jax.sharding import PartitionSpec as P

MESH = pl.DeviceIdType.MESH


def each(start, stop, body):
    def step(index, carry):
        body(index)
        return carry

    lax.fori_loop(start, stop, step, 0)


def exchange_kernel(
    n_shot, n_rcv,
    d_ref, s_ref, live_ref, o_ref, filt_ref,
    dbuf, pbuf, srec, live_v, rec, mbuf, fbuf, acc,
    load_sem, d_send, d_recv, r_send, p_send, p_recv, o_send, o_recv, f_send, f_recv,
):
    n_freq, own_rows = d_ref.shape[1], d_ref.shape[2]
    own_pts, own_shots = s_ref.shape[2], s_ref.shape[3]
    points = own_pts * n_rcv
    per_group = n_freq // n_rcv
    half = per_group // 2
    n_each = n_freq // (half * n_rcv)
    n_groups = n_shot // per_group
    n_dev = n_shot * n_rcv
    me_i, me_j = lax.axis_index("shot"), lax.axis_index("rcv")
    group, place = lax.div(me_i, per_group), lax.rem(me_i, per_group)
    me = me_i * n_rcv + me_j
    column = lax.rem(place, half)

    def base(g):
        return half * (1 - lax.rem(g, 2))

    computes = lax.div(place, half) == lax.div(base(group), half)

    load_s = pltpu.make_async_copy(s_ref, srec, load_sem.at[0])
    load_live = pltpu.make_async_copy(live_ref, live_v, load_sem.at[1])
    load_s.start()
    load_live.start()

    barrier = pltpu.get_barrier_semaphore()

    def greet(k):
        other = lax.rem(me + k, n_dev)
        pl.semaphore_signal(
            barrier, inc=1, device_id=(lax.div(other, n_rcv), lax.rem(other, n_rcv)), device_id_type=MESH
        )

    each(1, n_dev, greet)
    pl.semaphore_wait(barrier, n_dev - 1)

    def rows_of(i, size):
        return pl.ds(pl.multiple_of(i * size, size), size)

    def send(src, dst, target, send_sem, recv_sem):
        here = jnp.logical_and(target[0] == me_i, target[1] == me_j)

        @pl.when(here)
        def _():
            pltpu.make_async_copy(src, dst, recv_sem).start()

        @pl.when(jnp.logical_not(here))
        def _():
            pltpu.make_async_remote_copy(
                src_ref=src, dst_ref=dst, send_sem=send_sem, recv_sem=recv_sem,
                device_id=target, device_id_type=MESH,
            ).start()

    def sent(src, target, send_sem):
        here = jnp.logical_and(target[0] == me_i, target[1] == me_j)

        @pl.when(jnp.logical_not(here))
        def _():
            pltpu.make_async_copy(src, src, send_sem).wait()

    def arrived(dst, recv_sem):
        pltpu.make_async_copy(dst, dst, recv_sem).wait()

    def target_of(m):
        c = lax.rem(column + lax.div(m, n_rcv * n_each), half)
        j = lax.rem(me_j + lax.rem(lax.div(m, n_each), n_rcv), n_rcv)
        fi = lax.rem(m, n_each)
        return (group * per_group + base(group) + c, j), fi, (c * n_rcv + j) * n_each + fi

    def d_block(fi, i, j):
        return dbuf.at[fi, j, :, rows_of(i, own_rows), :]

    def send_d(m):
        target, fi, f = target_of(m)
        send(d_ref.at[:, f], d_block(fi, me_i, me_j), target, d_send.at[m], d_recv.at[fi, me_i, me_j])

    def sent_d(m):
        target, _, f = target_of(m)
        sent(d_ref.at[:, f], target, d_send.at[m])

    def send_p(m):
        target, fi, f = target_of(m)
        keep = live_v[...].astype(jnp.bfloat16)
        rec[f, :, :own_shots] = srec[0, f] * keep
        rec[f, :, own_shots:] = srec[1, f] * keep
        dst = pbuf.at[fi, place, rows_of(me_j, own_pts), :]
        send(rec.at[f], dst, target, p_send.at[m], p_recv.at[fi, place, me_j])

    def sent_p(m):
        target, _, f = target_of(m)
        sent(rec.at[f], target, p_send.at[m])

    @pl.when(computes)
    def _():
        each(0, n_freq, send_d)

    load_s.wait()
    load_live.wait()
    each(0, n_freq, send_p)

    first = n_freq - n_freq // 4

    @pl.when(jnp.logical_not(computes))
    def _():
        each(0, first, sent_p)
        each(0, n_freq, send_d)

    def partner(gg):
        g = lax.rem(group + gg, n_groups)
        return g, g * per_group + base(g) + column

    def position(g, t, far):
        near = base(g)
        return g * per_group + (half - near if far else near) + lax.rem(column + t, half)

    def relay_copy(fi, i, j, gg):
        _, target = partner(gg)
        return pltpu.make_async_remote_copy(
            src_ref=d_block(fi, i, j), dst_ref=d_block(fi, i, j),
            send_sem=r_send.at[gg - 1, fi, lax.rem(i, per_group), j], recv_sem=d_recv.at[fi, i, j],
            device_id=(target, me_j), device_id_type=MESH,
        )

    def relay(t, far, start, stop):
        i = position(group, t, far)

        def block(n):
            j = lax.rem(me_j + n_rcv - lax.div(n, n_each), n_rcv)
            fi = lax.rem(n, n_each)
            arrived(d_block(fi, i, j), d_recv.at[fi, i, j])
            each(1, n_groups, lambda gg: relay_copy(fi, i, j, gg).start())

        each(start * n_each, stop * n_each, block)

    def o_src(fi, b, i):
        return mbuf.at[fi, b, rows_of(i, own_rows), :]

    per_rcv = own_pts // own_rows

    def compute(i):
        rows = rows_of(i, own_rows)
        j = lax.div(i, per_rcv)

        def one(n):
            fi, b = lax.div(n, per_group), lax.rem(lax.rem(n, per_group) + place, per_group)
            total = None
            for h in range(n_rcv):
                block = pbuf[fi, b, h * own_pts:(h + 1) * own_pts, :]
                left = dbuf[fi, h, :, rows, :].reshape(2 * own_rows, own_pts)
                prod = jnp.dot(left, block, preferred_element_type=jnp.float32)
                total = prod if total is None else total + prod
            m_re = total[:own_rows, :own_shots] - total[own_rows:, own_shots:]
            m_im = total[:own_rows, own_shots:] + total[own_rows:, :own_shots]
            mbuf[fi, b, rows, :own_shots] = m_re.astype(jnp.bfloat16)
            mbuf[fi, b, rows, own_shots:] = m_im.astype(jnp.bfloat16)
            f = (column * n_rcv + me_j) * n_each + fi
            dst = o_ref.at[f, rows_of(lax.rem(i, per_rcv), own_rows), :]
            send(o_src(fi, b, i), dst, (group * per_group + b, j), o_send.at[fi, b, j], o_recv.at[f])
            p_re = pbuf[fi, b, rows, :own_shots].astype(jnp.float32)
            p_im = pbuf[fi, b, rows, own_shots:].astype(jnp.float32)

            def down(value):
                return jnp.sum(value.reshape(own_rows // 8, 8, own_shots), axis=0)

            acc[fi, b, 0] += down(m_re * p_re + m_im * p_im)
            acc[fi, b, 1] += down(m_re * p_im - m_im * p_re)
            acc[fi, b, 2] += down(m_re * m_re + m_im * m_im)

        each(0, n_each * per_group, one)

    def compute_others(t, far):
        def other(gg):
            g, _ = partner(gg)
            i = position(g, t, far)

            def block(n):
                j = lax.rem(me_j + n_rcv - lax.div(n, n_each), n_rcv)
                fi = lax.rem(n, n_each)
                arrived(d_block(fi, i, j), d_recv.at[fi, i, j])

            each(0, n_rcv * n_each, block)
            compute(i)

        each(1, n_groups, other)

    @pl.when(computes)
    def _():
        acc[...] = jnp.zeros_like(acc)
        for t in range(half):
            relay(t, False, 0, n_rcv)

        def records_arrived(n):
            fi, b, j = lax.div(n, per_group * n_rcv), lax.rem(lax.div(n, n_rcv), per_group), lax.rem(n, n_rcv)
            arrived(pbuf.at[fi, b, rows_of(j, own_pts), :], p_recv.at[fi, b, j])

        each(0, n_each * per_group * n_rcv, records_arrived)
        for t in range(half):
            compute(position(group, t, False))
        for t in range(half):
            compute_others(t, False)
        for t in range(half):
            relay(t, True, 0, n_rcv // 2)
            if t:
                compute_others(t - 1, True)
            relay(t, True, n_rcv // 2, n_rcv)
            compute(position(group, t, True))
        compute_others(half - 1, True)

        def f_args(n):
            fi, b, j = lax.div(n, per_group * n_rcv), lax.rem(lax.div(n, n_rcv), per_group), lax.rem(n, n_rcv)
            b = lax.rem(b + place, per_group)
            f = (column * n_rcv + me_j) * n_each + fi
            return fi, b, j, f, (group * per_group + b, j)

        def coefficients(n):
            fi, b = lax.div(n, per_group), lax.rem(n, per_group)
            num_re, num_im, power = (
                jnp.sum(acc[fi, b, v], axis=0, keepdims=True) / float(points) for v in range(3)
            )
            power = power + 1e-6
            row = lax.broadcasted_iota(jnp.int32, (8, own_shots), 0)
            fbuf[fi, b] = jnp.where(row < 4, num_re / power, num_im / power)

        each(0, n_each * per_group, coefficients)

        def send_f(n):
            fi, b, j, f, target = f_args(n)
            send(fbuf.at[fi, b], filt_ref.at[f], target, f_send.at[fi, b, j], f_recv.at[f])

        each(0, n_each * per_group * n_rcv, send_f)

        def sent_results(n):
            fi, b, j, _, target = f_args(n)
            sent(fbuf.at[fi, b], target, f_send.at[fi, b, j])
            sent(mbuf.at[fi, b, rows_of(j, own_pts), :], target, o_send.at[fi, b, j])

        each(0, n_each * per_group * n_rcv, sent_results)

        def sent_relays(n):
            gg = lax.div(n, n_each * per_group * n_rcv) + 1
            fi = lax.rem(lax.div(n, per_group * n_rcv), n_each)
            b, j = lax.rem(lax.div(n, n_rcv), per_group), lax.rem(n, n_rcv)
            relay_copy(fi, group * per_group + b, j, gg).wait_send()

        each(0, (n_groups - 1) * n_each * per_group * n_rcv, sent_relays)
        each(0, first, sent_p)

    def result_arrived(n):
        arrived(o_ref.at[n], o_recv.at[n])
        arrived(filt_ref.at[n], f_recv.at[n])

    each(0, n_freq, result_arrived)
    each(0, n_freq, sent_d)
    each(first, n_freq, sent_p)


def subtract_kernel(o_ref, filt_ref, s_ref, live_ref, pred_ref, prim_ref):
    shots = s_ref.shape[3]
    keep = live_ref[...].astype(jnp.bfloat16)
    for f in range(o_ref.shape[0]):
        re, im = o_ref[f, :, :shots], o_ref[f, :, shots:]
        pred_ref[0, f] = re
        pred_ref[1, f] = im
        re, im = re.astype(jnp.float32), im.astype(jnp.float32)
        filt_re, filt_im = filt_ref[f, 0:1, :], filt_ref[f, 4:5, :]
        rec_re = (s_ref[0, f] * keep).astype(jnp.float32)
        rec_im = (s_ref[1, f] * keep).astype(jnp.float32)
        prim_ref[0, f] = (rec_re - (filt_re * re - filt_im * im)).astype(jnp.bfloat16)
        prim_ref[1, f] = (rec_im - (filt_re * im + filt_im * re)).astype(jnp.bfloat16)


def shards(n_shot, n_rcv, data_matrix, shot_records, live):
    _, n_freq, own_rows, own_pts = data_matrix.shape
    own_shots = shot_records.shape[3]
    points = own_pts * n_rcv
    per_group = n_freq // n_rcv
    n_groups = n_shot // per_group
    n_each = n_freq // (per_group // 2 * n_rcv)
    anywhere = pl.BlockSpec(memory_space=pl.ANY)
    dma = pltpu.SemaphoreType.DMA
    multiples, filt = pl.pallas_call(
        functools.partial(exchange_kernel, n_shot, n_rcv),
        out_shape=(
            jax.ShapeDtypeStruct((n_freq, own_pts, 2 * own_shots), jnp.bfloat16),
            jax.ShapeDtypeStruct((n_freq, 8, own_shots), jnp.float32),
        ),
        in_specs=[anywhere] * 3,
        out_specs=(anywhere, anywhere),
        scratch_shapes=[
            pltpu.VMEM((n_each, n_rcv, 2, points, own_pts), jnp.bfloat16),
            pltpu.VMEM((n_each, per_group, points, 2 * own_shots), jnp.bfloat16),
            pltpu.VMEM((2, n_freq, own_pts, own_shots), jnp.bfloat16),
            pltpu.VMEM((own_pts, own_shots), jnp.int32),
            pltpu.VMEM((n_freq, own_pts, 2 * own_shots), jnp.bfloat16),
            pltpu.VMEM((n_each, per_group, points, 2 * own_shots), jnp.bfloat16),
            pltpu.VMEM((n_each, per_group, 8, own_shots), jnp.float32),
            pltpu.VMEM((n_each, per_group, 3, 8, own_shots), jnp.float32),
            dma((2,)),
            dma((n_freq,)),
            dma((n_each, n_shot, n_rcv)),
            dma((n_groups - 1, n_each, per_group, n_rcv)),
            dma((n_freq,)),
            dma((n_each, per_group, n_rcv)),
            dma((n_each, per_group, n_rcv)),
            dma((n_freq,)),
            dma((n_each, per_group, n_rcv)),
            dma((n_freq,)),
        ],
        compiler_params=pltpu.CompilerParams(
            collective_id=0, has_side_effects=True, vmem_limit_bytes=40 * 1024 * 1024
        ),
    )(data_matrix, shot_records, live)
    step = 4
    pair = pl.BlockSpec((2, step, own_pts, own_shots), lambda f: (0, f, 0, 0))
    out = jax.ShapeDtypeStruct((2, n_freq, own_pts, own_shots), jnp.bfloat16)
    return pl.pallas_call(
        subtract_kernel,
        grid=(n_freq // step,),
        out_shape=(out, out),
        in_specs=[
            pl.BlockSpec((step, own_pts, 2 * own_shots), lambda f: (f, 0, 0)),
            pl.BlockSpec((step, 8, own_shots), lambda f: (f, 0, 0)),
            pair,
            pl.BlockSpec((own_pts, own_shots), lambda f: (0, 0)),
        ],
        out_specs=(pair, pair),
        compiler_params=pltpu.CompilerParams(vmem_limit_bytes=24 * 1024 * 1024),
    )(multiples, filt, shot_records, live)


def solution(mesh):
    in_specs = (P(None, None, "shot", "rcv"), P(None, None, "rcv", "shot"), P("rcv", "shot"))
    out_specs = (P(None, None, "rcv", "shot"), P(None, None, "rcv", "shot"))
    body = functools.partial(shards, mesh.shape["shot"], mesh.shape["rcv"])
    return jax.shard_map(body, mesh=mesh, in_specs=in_specs, out_specs=out_specs, check_vma=False)
```

```python
import functools

import jax
import jax.numpy as jnp
from jax import lax
from jax.experimental import pallas as pl
from jax.experimental.pallas import tpu as pltpu
from jax.sharding import PartitionSpec as P

MESH = pl.DeviceIdType.MESH


def each(start, stop, body):
    def step(index, carry):
        body(index)
        return carry

    lax.fori_loop(start, stop, step, 0)


def exchange_kernel(
    n_shot, n_rcv,
    d_ref, s_ref, live_ref, o_ref, filt_ref,
    dbuf, pbuf, srec, live_v, rec, mbuf, fbuf, acc,
    load_sem, d_send, d_recv, p_send, p_recv, o_send, o_recv, f_send, f_recv,
):
    n_freq, own_rows = d_ref.shape[1], d_ref.shape[2]
    own_pts, own_shots = s_ref.shape[2], s_ref.shape[3]
    points = own_pts * n_rcv
    per_group = n_freq // n_rcv
    n_groups = n_shot // per_group
    n_dev = n_shot * n_rcv
    me_i, me_j = lax.axis_index("shot"), lax.axis_index("rcv")
    group, place = lax.div(me_i, per_group), lax.rem(me_i, per_group)
    me = me_i * n_rcv + me_j
    my_f = place * n_rcv + me_j

    load_s = pltpu.make_async_copy(s_ref, srec, load_sem.at[0])
    load_live = pltpu.make_async_copy(live_ref, live_v, load_sem.at[1])
    load_s.start()
    load_live.start()

    barrier = pltpu.get_barrier_semaphore()

    def greet(k):
        other = lax.rem(me + k, n_dev)
        pl.semaphore_signal(
            barrier, inc=1, device_id=(lax.div(other, n_rcv), lax.rem(other, n_rcv)), device_id_type=MESH
        )

    each(1, n_dev, greet)
    pl.semaphore_wait(barrier, n_dev - 1)

    def rows_of(i, size):
        return pl.ds(pl.multiple_of(i * size, size), size)

    def send(src, dst, target, send_sem, recv_sem):
        here = jnp.logical_and(target[0] == me_i, target[1] == me_j)

        @pl.when(here)
        def _():
            pltpu.make_async_copy(src, dst, recv_sem).start()

        @pl.when(jnp.logical_not(here))
        def _():
            pltpu.make_async_remote_copy(
                src_ref=src, dst_ref=dst, send_sem=send_sem, recv_sem=recv_sem,
                device_id=target, device_id_type=MESH,
            ).start()

    def sent(src, target, send_sem):
        here = jnp.logical_and(target[0] == me_i, target[1] == me_j)

        @pl.when(jnp.logical_not(here))
        def _():
            pltpu.make_async_copy(src, src, send_sem).wait()

    def arrived(dst, recv_sem):
        pltpu.make_async_copy(dst, dst, recv_sem).wait()

    def target_of(k):
        p = lax.rem(place + lax.div(k, n_rcv), per_group)
        j = lax.rem(me_j + lax.rem(k, n_rcv), n_rcv)
        return p, j, p * n_rcv + j

    def d_block(i, j):
        return dbuf.at[j, :, rows_of(i, own_rows), :]

    def d_target(k, gg):
        p, j, f = target_of(k)
        return (lax.rem(group + gg, n_groups) * per_group + p, j), f

    def send_d(k, gg):
        target, f = d_target(k, gg)
        send(d_ref.at[:, f], d_block(me_i, me_j), target, d_send.at[gg, k], d_recv.at[me_i, me_j])

    def sent_d(n):
        gg, k = lax.div(n, n_freq), lax.rem(n, n_freq)
        target, f = d_target(k, gg)
        sent(d_ref.at[:, f], target, d_send.at[gg, k])

    def send_d_others(k):
        each(1, n_groups, lambda gg: send_d(k, gg))

    def send_p(k):
        p, j, f = target_of(k)
        keep = live_v[...].astype(jnp.bfloat16)
        rec[f, :, :own_shots] = srec[0, f] * keep
        rec[f, :, own_shots:] = srec[1, f] * keep
        dst = pbuf.at[place, rows_of(me_j, own_pts), :]
        send(rec.at[f], dst, (group * per_group + p, j), p_send.at[k], p_recv.at[place, me_j])

    def sent_p(k):
        p, j, f = target_of(k)
        sent(rec.at[f], (group * per_group + p, j), p_send.at[k])

    early, middle = 2, n_freq // 2
    each(0, early, send_d_others)
    load_s.wait()
    load_live.wait()

    def send_first(k):
        send_p(2 * k)
        send_p(2 * k + 1)
        send_d_others(k + early)

    def send_own(k):
        send_d(2 * (k - middle), 0)
        send_d(2 * (k - middle) + 1, 0)

    def send_second(k):
        send_own(k)
        send_d_others(k + early)

    each(0, middle, send_first)
    each(middle, n_freq - early, send_second)
    each(n_freq - early, n_freq, send_own)

    def records_arrived(n):
        b, j = lax.div(n, n_rcv), lax.rem(n, n_rcv)
        arrived(pbuf.at[b, rows_of(j, own_pts), :], p_recv.at[b, j])

    acc[...] = jnp.zeros_like(acc)
    each(0, n_freq, records_arrived)

    def o_src(b, i):
        return mbuf.at[b, rows_of(i, own_rows), :]

    per_rcv = own_pts // own_rows

    def compute(i):
        rows = rows_of(i, own_rows)
        j = lax.div(i, per_rcv)

        def arrival(h):
            arrived(d_block(i, h), d_recv.at[i, h])

        each(0, n_rcv, arrival)

        def one(n):
            b = lax.rem(n + place, per_group)
            total = None
            for h in range(n_rcv):
                block = pbuf[b, h * own_pts:(h + 1) * own_pts, :]
                left = dbuf[h, :, rows, :].reshape(2 * own_rows, own_pts)
                prod = jnp.dot(left, block, preferred_element_type=jnp.float32)
                total = prod if total is None else total + prod
            m_re = total[:own_rows, :own_shots] - total[own_rows:, own_shots:]
            m_im = total[:own_rows, own_shots:] + total[own_rows:, :own_shots]
            mbuf[b, rows, :own_shots] = m_re.astype(jnp.bfloat16)
            mbuf[b, rows, own_shots:] = m_im.astype(jnp.bfloat16)
            dst = o_ref.at[my_f, rows_of(lax.rem(i, per_rcv), own_rows), :]
            send(o_src(b, i), dst, (group * per_group + b, j), o_send.at[b, j], o_recv.at[my_f])
            p_re = pbuf[b, rows, :own_shots].astype(jnp.float32)
            p_im = pbuf[b, rows, own_shots:].astype(jnp.float32)

            def down(value):
                return jnp.sum(value.reshape(own_rows // 8, 8, own_shots), axis=0)

            acc[b, 0] += down(m_re * p_re + m_im * p_im)
            acc[b, 1] += down(m_re * p_im - m_im * p_re)
            acc[b, 2] += down(m_re * m_re + m_im * m_im)

        each(0, per_group, one)

    turns = [((t + 1) * n_rcv, 0, t) for t in range(per_group)]
    turns += [(middle + (t + 1) * n_rcv // 2, 1, t) for t in range(per_group)]
    for _, own, t in sorted(turns):
        p = lax.rem(place + per_group - t, per_group)
        if own:
            compute(group * per_group + p)
        else:
            each(1, n_groups, lambda gg: compute(lax.rem(group + gg, n_groups) * per_group + p))

    def coefficients(n):
        b = lax.rem(n + place, per_group)
        num_re, num_im, power = (
            jnp.sum(acc[b, v], axis=0, keepdims=True) / float(points) for v in range(3)
        )
        power = power + 1e-6
        row = lax.broadcasted_iota(jnp.int32, (8, own_shots), 0)
        fbuf[b] = jnp.where(row < 4, num_re / power, num_im / power)
        for j in range(n_rcv):
            send(fbuf.at[b], filt_ref.at[my_f], (group * per_group + b, j), f_send.at[b, j], f_recv.at[my_f])

    each(0, per_group, coefficients)

    def sent_results(n):
        b, j = lax.div(n, n_rcv), lax.rem(n, n_rcv)
        target = (group * per_group + b, j)
        sent(fbuf.at[b], target, f_send.at[b, j])
        sent(mbuf.at[b, rows_of(j, own_pts), :], target, o_send.at[b, j])

    def result_arrived(n):
        arrived(o_ref.at[n], o_recv.at[n])
        arrived(filt_ref.at[n], f_recv.at[n])

    each(0, n_freq, result_arrived)
    each(0, n_freq * n_groups, sent_d)
    each(0, n_freq, sent_p)
    each(0, per_group * n_rcv, sent_results)


def subtract_kernel(o_ref, filt_ref, s_ref, live_ref, pred_ref, prim_ref):
    shots = s_ref.shape[3]
    keep = live_ref[...].astype(jnp.bfloat16)
    for f in range(o_ref.shape[0]):
        re, im = o_ref[f, :, :shots], o_ref[f, :, shots:]
        pred_ref[0, f] = re
        pred_ref[1, f] = im
        re, im = re.astype(jnp.float32), im.astype(jnp.float32)
        filt_re, filt_im = filt_ref[f, 0:1, :], filt_ref[f, 4:5, :]
        rec_re = (s_ref[0, f] * keep).astype(jnp.float32)
        rec_im = (s_ref[1, f] * keep).astype(jnp.float32)
        prim_ref[0, f] = (rec_re - (filt_re * re - filt_im * im)).astype(jnp.bfloat16)
        prim_ref[1, f] = (rec_im - (filt_re * im + filt_im * re)).astype(jnp.bfloat16)


def shards(n_shot, n_rcv, data_matrix, shot_records, live):
    _, n_freq, own_rows, own_pts = data_matrix.shape
    own_shots = shot_records.shape[3]
    points = own_pts * n_rcv
    per_group = n_freq // n_rcv
    n_groups = n_shot // per_group
    anywhere = pl.BlockSpec(memory_space=pl.ANY)
    dma = pltpu.SemaphoreType.DMA
    multiples, filt = pl.pallas_call(
        functools.partial(exchange_kernel, n_shot, n_rcv),
        out_shape=(
            jax.ShapeDtypeStruct((n_freq, own_pts, 2 * own_shots), jnp.bfloat16),
            jax.ShapeDtypeStruct((n_freq, 8, own_shots), jnp.float32),
        ),
        in_specs=[anywhere] * 3,
        out_specs=(anywhere, anywhere),
        scratch_shapes=[
            pltpu.VMEM((n_rcv, 2, points, own_pts), jnp.bfloat16),
            pltpu.VMEM((per_group, points, 2 * own_shots), jnp.bfloat16),
            pltpu.VMEM((2, n_freq, own_pts, own_shots), jnp.bfloat16),
            pltpu.VMEM((own_pts, own_shots), jnp.int32),
            pltpu.VMEM((n_freq, own_pts, 2 * own_shots), jnp.bfloat16),
            pltpu.VMEM((per_group, points, 2 * own_shots), jnp.bfloat16),
            pltpu.VMEM((per_group, 8, own_shots), jnp.float32),
            pltpu.VMEM((per_group, 3, 8, own_shots), jnp.float32),
            dma((2,)),
            dma((n_groups, n_freq)),
            dma((n_shot, n_rcv)),
            dma((n_freq,)),
            dma((per_group, n_rcv)),
            dma((per_group, n_rcv)),
            dma((n_freq,)),
            dma((per_group, n_rcv)),
            dma((n_freq,)),
        ],
        compiler_params=pltpu.CompilerParams(
            collective_id=0, has_side_effects=True, vmem_limit_bytes=60 * 1024 * 1024
        ),
    )(data_matrix, shot_records, live)
    step = 4
    pair = pl.BlockSpec((2, step, own_pts, own_shots), lambda f: (0, f, 0, 0))
    out = jax.ShapeDtypeStruct((2, n_freq, own_pts, own_shots), jnp.bfloat16)
    return pl.pallas_call(
        subtract_kernel,
        grid=(n_freq // step,),
        out_shape=(out, out),
        in_specs=[
            pl.BlockSpec((step, own_pts, 2 * own_shots), lambda f: (f, 0, 0)),
            pl.BlockSpec((step, 8, own_shots), lambda f: (f, 0, 0)),
            pair,
            pl.BlockSpec((own_pts, own_shots), lambda f: (0, 0)),
        ],
        out_specs=(pair, pair),
        compiler_params=pltpu.CompilerParams(vmem_limit_bytes=24 * 1024 * 1024),
    )(multiples, filt, shot_records, live)


def solution(mesh):
    in_specs = (P(None, None, "shot", "rcv"), P(None, None, "rcv", "shot"), P("rcv", "shot"))
    out_specs = (P(None, None, "rcv", "shot"), P(None, None, "rcv", "shot"))
    body = functools.partial(shards, mesh.shape["shot"], mesh.shape["rcv"])
    return jax.shard_map(body, mesh=mesh, in_specs=in_specs, out_specs=out_specs, check_vma=False)
```

```python
import functools

import jax
import jax.numpy as jnp
from jax import lax
from jax.experimental import pallas as pl
from jax.experimental.pallas import tpu as pltpu
from jax.sharding import PartitionSpec as P

MESH = pl.DeviceIdType.MESH


def each(start, stop, body):
    def step(index, carry):
        body(index)
        return carry

    lax.fori_loop(start, stop, step, 0)


def exchange_kernel(
    n_shot, n_rcv,
    d_ref, s_ref, live_ref, o_ref, filt_ref,
    dbuf, pbuf, srec, live_v, rec, mbuf, fbuf, acc,
    load_sem, d_send, d_recv, p_send, p_recv, o_send, o_recv, f_send, f_recv,
):
    n_freq, own_rows = d_ref.shape[1], d_ref.shape[2]
    own_pts, own_shots = s_ref.shape[2], s_ref.shape[3]
    points = own_pts * n_rcv
    per_group = n_freq // n_rcv
    n_groups = n_shot // per_group
    n_dev = n_shot * n_rcv
    me_i, me_j = lax.axis_index("shot"), lax.axis_index("rcv")
    group, place = lax.div(me_i, per_group), lax.rem(me_i, per_group)
    me = me_i * n_rcv + me_j
    my_f = place * n_rcv + me_j

    load_s = pltpu.make_async_copy(s_ref, srec, load_sem.at[0])
    load_live = pltpu.make_async_copy(live_ref, live_v, load_sem.at[1])
    load_s.start()
    load_live.start()

    barrier = pltpu.get_barrier_semaphore()

    def greet(k):
        other = lax.rem(me + k, n_dev)
        pl.semaphore_signal(
            barrier, inc=1, device_id=(lax.div(other, n_rcv), lax.rem(other, n_rcv)), device_id_type=MESH
        )

    each(1, n_dev, greet)
    pl.semaphore_wait(barrier, n_dev - 1)

    def rows_of(i, size):
        return pl.ds(pl.multiple_of(i * size, size), size)

    def send(src, dst, target, send_sem, recv_sem):
        here = jnp.logical_and(target[0] == me_i, target[1] == me_j)

        @pl.when(here)
        def _():
            pltpu.make_async_copy(src, dst, recv_sem).start()

        @pl.when(jnp.logical_not(here))
        def _():
            pltpu.make_async_remote_copy(
                src_ref=src, dst_ref=dst, send_sem=send_sem, recv_sem=recv_sem,
                device_id=target, device_id_type=MESH,
            ).start()

    def sent(src, target, send_sem):
        here = jnp.logical_and(target[0] == me_i, target[1] == me_j)

        @pl.when(jnp.logical_not(here))
        def _():
            pltpu.make_async_copy(src, src, send_sem).wait()

    def arrived(dst, recv_sem):
        pltpu.make_async_copy(dst, dst, recv_sem).wait()

    def target_of(k):
        p = lax.rem(place + lax.div(k, n_rcv), per_group)
        j = lax.rem(me_j + lax.rem(k, n_rcv), n_rcv)
        return p, j, p * n_rcv + j

    def d_block(i, j):
        return dbuf.at[j, :, rows_of(i, own_rows), :]

    def d_target(k, gg):
        p, j, f = target_of(k)
        return (lax.rem(group + gg, n_groups) * per_group + p, j), f

    def send_d(k, gg):
        target, f = d_target(k, gg)
        send(d_ref.at[:, f], d_block(me_i, me_j), target, d_send.at[gg, k], d_recv.at[me_i, me_j])

    def sent_d(n):
        gg, k = lax.div(n, n_freq), lax.rem(n, n_freq)
        target, f = d_target(k, gg)
        sent(d_ref.at[:, f], target, d_send.at[gg, k])

    def send_d_others(k):
        each(1, n_groups, lambda gg: send_d(k, gg))

    def send_p(k):
        p, j, f = target_of(k)
        keep = live_v[...].astype(jnp.bfloat16)
        rec[f, :, :own_shots] = srec[0, f] * keep
        rec[f, :, own_shots:] = srec[1, f] * keep
        dst = pbuf.at[place, rows_of(me_j, own_pts), :]
        send(rec.at[f], dst, (group * per_group + p, j), p_send.at[k], p_recv.at[place, me_j])

    def sent_p(k):
        p, j, f = target_of(k)
        sent(rec.at[f], (group * per_group + p, j), p_send.at[k])

    early, middle = 2, n_freq // 2
    each(0, early, send_d_others)
    load_s.wait()
    load_live.wait()

    def send_records(k):
        send_p(2 * k)
        send_p(2 * k + 1)
        send_d_others(k + early)
        send_d(k, 0)

    def send_rest(k):
        send_d_others(k + early)
        send_d(k, 0)

    each(0, middle, send_records)
    each(middle, n_freq - early, send_rest)
    each(n_freq - early, n_freq, lambda k: send_d(k, 0))

    def records_arrived(n):
        b, j = lax.div(n, n_rcv), lax.rem(n, n_rcv)
        arrived(pbuf.at[b, rows_of(j, own_pts), :], p_recv.at[b, j])

    acc[...] = jnp.zeros_like(acc)
    each(0, n_freq, records_arrived)

    def o_src(b, i):
        return mbuf.at[b, rows_of(i, own_rows), :]

    per_rcv = own_pts // own_rows

    def compute(i):
        rows = rows_of(i, own_rows)
        j = lax.div(i, per_rcv)

        def arrival(h):
            arrived(d_block(i, h), d_recv.at[i, h])

        each(0, n_rcv, arrival)

        def one(n):
            b = lax.rem(n + place, per_group)
            total = None
            for h in range(n_rcv):
                block = pbuf[b, h * own_pts:(h + 1) * own_pts, :]
                left = dbuf[h, :, rows, :].reshape(2 * own_rows, own_pts)
                prod = jnp.dot(left, block, preferred_element_type=jnp.float32)
                total = prod if total is None else total + prod
            m_re = total[:own_rows, :own_shots] - total[own_rows:, own_shots:]
            m_im = total[:own_rows, own_shots:] + total[own_rows:, :own_shots]
            mbuf[b, rows, :own_shots] = m_re.astype(jnp.bfloat16)
            mbuf[b, rows, own_shots:] = m_im.astype(jnp.bfloat16)
            dst = o_ref.at[my_f, rows_of(lax.rem(i, per_rcv), own_rows), :]
            send(o_src(b, i), dst, (group * per_group + b, j), o_send.at[b, j], o_recv.at[my_f])
            p_re = pbuf[b, rows, :own_shots].astype(jnp.float32)
            p_im = pbuf[b, rows, own_shots:].astype(jnp.float32)

            def down(value):
                return jnp.sum(value.reshape(own_rows // 8, 8, own_shots), axis=0)

            acc[b, 0] += down(m_re * p_re + m_im * p_im)
            acc[b, 1] += down(m_re * p_im - m_im * p_re)
            acc[b, 2] += down(m_re * m_re + m_im * m_im)

        each(0, per_group, one)

    turns = [((t + 1) * n_rcv, 0, t) for t in range(per_group)]
    turns += [((t + 1) * n_rcv, 1, t) for t in range(per_group)]
    for _, own, t in sorted(turns):
        p = lax.rem(place + per_group - t, per_group)
        if own:
            compute(group * per_group + p)
        else:
            each(1, n_groups, lambda gg: compute(lax.rem(group + gg, n_groups) * per_group + p))

    def coefficients(n):
        b = lax.rem(n + place, per_group)
        num_re, num_im, power = (
            jnp.sum(acc[b, v], axis=0, keepdims=True) / float(points) for v in range(3)
        )
        power = power + 1e-6
        row = lax.broadcasted_iota(jnp.int32, (8, own_shots), 0)
        fbuf[b] = jnp.where(row < 4, num_re / power, num_im / power)
        for j in range(n_rcv):
            send(fbuf.at[b], filt_ref.at[my_f], (group * per_group + b, j), f_send.at[b, j], f_recv.at[my_f])

    each(0, per_group, coefficients)

    def sent_results(n):
        b, j = lax.div(n, n_rcv), lax.rem(n, n_rcv)
        target = (group * per_group + b, j)
        sent(fbuf.at[b], target, f_send.at[b, j])
        sent(mbuf.at[b, rows_of(j, own_pts), :], target, o_send.at[b, j])

    def result_arrived(n):
        arrived(o_ref.at[n], o_recv.at[n])
        arrived(filt_ref.at[n], f_recv.at[n])

    each(0, n_freq, result_arrived)
    each(0, n_freq * n_groups, sent_d)
    each(0, n_freq, sent_p)
    each(0, per_group * n_rcv, sent_results)


def subtract_kernel(o_ref, filt_ref, s_ref, live_ref, pred_ref, prim_ref):
    shots = s_ref.shape[3]
    keep = live_ref[...].astype(jnp.bfloat16)
    for f in range(o_ref.shape[0]):
        re, im = o_ref[f, :, :shots], o_ref[f, :, shots:]
        pred_ref[0, f] = re
        pred_ref[1, f] = im
        re, im = re.astype(jnp.float32), im.astype(jnp.float32)
        filt_re, filt_im = filt_ref[f, 0:1, :], filt_ref[f, 4:5, :]
        rec_re = (s_ref[0, f] * keep).astype(jnp.float32)
        rec_im = (s_ref[1, f] * keep).astype(jnp.float32)
        prim_ref[0, f] = (rec_re - (filt_re * re - filt_im * im)).astype(jnp.bfloat16)
        prim_ref[1, f] = (rec_im - (filt_re * im + filt_im * re)).astype(jnp.bfloat16)


def shards(n_shot, n_rcv, data_matrix, shot_records, live):
    _, n_freq, own_rows, own_pts = data_matrix.shape
    own_shots = shot_records.shape[3]
    points = own_pts * n_rcv
    per_group = n_freq // n_rcv
    n_groups = n_shot // per_group
    anywhere = pl.BlockSpec(memory_space=pl.ANY)
    dma = pltpu.SemaphoreType.DMA
    multiples, filt = pl.pallas_call(
        functools.partial(exchange_kernel, n_shot, n_rcv),
        out_shape=(
            jax.ShapeDtypeStruct((n_freq, own_pts, 2 * own_shots), jnp.bfloat16),
            jax.ShapeDtypeStruct((n_freq, 8, own_shots), jnp.float32),
        ),
        in_specs=[anywhere] * 3,
        out_specs=(anywhere, anywhere),
        scratch_shapes=[
            pltpu.VMEM((n_rcv, 2, points, own_pts), jnp.bfloat16),
            pltpu.VMEM((per_group, points, 2 * own_shots), jnp.bfloat16),
            pltpu.VMEM((2, n_freq, own_pts, own_shots), jnp.bfloat16),
            pltpu.VMEM((own_pts, own_shots), jnp.int32),
            pltpu.VMEM((n_freq, own_pts, 2 * own_shots), jnp.bfloat16),
            pltpu.VMEM((per_group, points, 2 * own_shots), jnp.bfloat16),
            pltpu.VMEM((per_group, 8, own_shots), jnp.float32),
            pltpu.VMEM((per_group, 3, 8, own_shots), jnp.float32),
            dma((2,)),
            dma((n_groups, n_freq)),
            dma((n_shot, n_rcv)),
            dma((n_freq,)),
            dma((per_group, n_rcv)),
            dma((per_group, n_rcv)),
            dma((n_freq,)),
            dma((per_group, n_rcv)),
            dma((n_freq,)),
        ],
        compiler_params=pltpu.CompilerParams(
            collective_id=0, has_side_effects=True, vmem_limit_bytes=60 * 1024 * 1024
        ),
    )(data_matrix, shot_records, live)
    step = 4
    pair = pl.BlockSpec((2, step, own_pts, own_shots), lambda f: (0, f, 0, 0))
    out = jax.ShapeDtypeStruct((2, n_freq, own_pts, own_shots), jnp.bfloat16)
    return pl.pallas_call(
        subtract_kernel,
        grid=(n_freq // step,),
        out_shape=(out, out),
        in_specs=[
            pl.BlockSpec((step, own_pts, 2 * own_shots), lambda f: (f, 0, 0)),
            pl.BlockSpec((step, 8, own_shots), lambda f: (f, 0, 0)),
            pair,
            pl.BlockSpec((own_pts, own_shots), lambda f: (0, 0)),
        ],
        out_specs=(pair, pair),
        compiler_params=pltpu.CompilerParams(vmem_limit_bytes=24 * 1024 * 1024),
    )(multiples, filt, shot_records, live)


def solution(mesh):
    in_specs = (P(None, None, "shot", "rcv"), P(None, None, "rcv", "shot"), P("rcv", "shot"))
    out_specs = (P(None, None, "rcv", "shot"), P(None, None, "rcv", "shot"))
    body = functools.partial(shards, mesh.shape["shot"], mesh.shape["rcv"])
    return jax.shard_map(body, mesh=mesh, in_specs=in_specs, out_specs=out_specs, check_vma=False)
```

```python
import functools

import jax
import jax.numpy as jnp
from jax import lax
from jax.experimental import pallas as pl
from jax.experimental.pallas import tpu as pltpu
from jax.sharding import PartitionSpec as P

MESH = pl.DeviceIdType.MESH


def each(start, stop, body):
    def step(index, carry):
        body(index)
        return carry

    lax.fori_loop(start, stop, step, 0)


def exchange_kernel(
    n_shot, n_rcv,
    d_ref, s_ref, live_ref, o_ref, filt_ref,
    dbuf, pbuf, srec, live_v, rec, mbuf, fbuf, acc,
    load_sem, d_send, d_recv, p_send, p_recv, o_send, o_recv, f_send, f_recv,
):
    n_freq, own_rows = d_ref.shape[1], d_ref.shape[2]
    own_pts, own_shots = s_ref.shape[2], s_ref.shape[3]
    points = own_pts * n_rcv
    per_group = n_freq // n_rcv
    n_groups = n_shot // per_group
    n_dev = n_shot * n_rcv
    me_i, me_j = lax.axis_index("shot"), lax.axis_index("rcv")
    group, place = lax.div(me_i, per_group), lax.rem(me_i, per_group)
    me = me_i * n_rcv + me_j
    my_f = place * n_rcv + me_j

    load_s = pltpu.make_async_copy(s_ref, srec, load_sem.at[0])
    load_live = pltpu.make_async_copy(live_ref, live_v, load_sem.at[1])
    load_s.start()
    load_live.start()

    barrier = pltpu.get_barrier_semaphore()

    def greet(k):
        other = lax.rem(me + k, n_dev)
        pl.semaphore_signal(
            barrier, inc=1, device_id=(lax.div(other, n_rcv), lax.rem(other, n_rcv)), device_id_type=MESH
        )

    each(1, n_dev, greet)
    pl.semaphore_wait(barrier, n_dev - 1)

    def rows_of(i, size):
        return pl.ds(pl.multiple_of(i * size, size), size)

    def send(src, dst, target, send_sem, recv_sem):
        here = jnp.logical_and(target[0] == me_i, target[1] == me_j)

        @pl.when(here)
        def _():
            pltpu.make_async_copy(src, dst, recv_sem).start()

        @pl.when(jnp.logical_not(here))
        def _():
            pltpu.make_async_remote_copy(
                src_ref=src, dst_ref=dst, send_sem=send_sem, recv_sem=recv_sem,
                device_id=target, device_id_type=MESH,
            ).start()

    def sent(src, target, send_sem):
        here = jnp.logical_and(target[0] == me_i, target[1] == me_j)

        @pl.when(jnp.logical_not(here))
        def _():
            pltpu.make_async_copy(src, src, send_sem).wait()

    def arrived(dst, recv_sem):
        pltpu.make_async_copy(dst, dst, recv_sem).wait()

    def target_of(k):
        p = lax.rem(place + lax.div(k, n_rcv), per_group)
        j = lax.rem(me_j + lax.rem(k, n_rcv), n_rcv)
        return p, j, p * n_rcv + j

    def d_block(i, j):
        return dbuf.at[j, :, rows_of(i, own_rows), :]

    def d_target(k, gg):
        p, j, f = target_of(k)
        return (lax.rem(group + gg, n_groups) * per_group + p, j), f

    def send_d(k, gg):
        target, f = d_target(k, gg)
        send(d_ref.at[:, f], d_block(me_i, me_j), target, d_send.at[gg, k], d_recv.at[me_i, me_j])

    def sent_d(n):
        gg, k = lax.div(n, n_freq), lax.rem(n, n_freq)
        target, f = d_target(k, gg)
        sent(d_ref.at[:, f], target, d_send.at[gg, k])

    def send_d_others(k):
        each(1, n_groups, lambda gg: send_d(k, gg))

    def send_p(k):
        p, j, f = target_of(k)
        keep = live_v[...].astype(jnp.bfloat16)
        rec[f, :, :own_shots] = srec[0, f] * keep
        rec[f, :, own_shots:] = srec[1, f] * keep
        dst = pbuf.at[place, rows_of(me_j, own_pts), :]
        send(rec.at[f], dst, (group * per_group + p, j), p_send.at[k], p_recv.at[place, me_j])

    def sent_p(k):
        p, j, f = target_of(k)
        sent(rec.at[f], (group * per_group + p, j), p_send.at[k])

    early = 2
    each(0, early, send_d_others)
    load_s.wait()
    load_live.wait()

    def send_records(k):
        for n in range(4):
            send_p(4 * k + n)
        send_d_others(k + early)
        send_d(k, 0)

    def send_rest(k):
        send_d_others(k + early)
        send_d(k, 0)

    each(0, n_freq // 4, send_records)
    each(n_freq // 4, n_freq - early, send_rest)
    each(n_freq - early, n_freq, lambda k: send_d(k, 0))

    def records_arrived(n):
        b, j = lax.div(n, n_rcv), lax.rem(n, n_rcv)
        arrived(pbuf.at[b, rows_of(j, own_pts), :], p_recv.at[b, j])

    acc[...] = jnp.zeros_like(acc)
    each(0, n_freq, records_arrived)

    def o_src(b, i):
        return mbuf.at[b, rows_of(i, own_rows), :]

    per_rcv = own_pts // own_rows

    def compute(i):
        rows = rows_of(i, own_rows)
        j = lax.div(i, per_rcv)

        def arrival(h):
            arrived(d_block(i, h), d_recv.at[i, h])

        each(0, n_rcv, arrival)

        def one(n):
            b = lax.rem(n + place, per_group)
            total = None
            for h in range(n_rcv):
                block = pbuf[b, h * own_pts:(h + 1) * own_pts, :]
                left = dbuf[h, :, rows, :].reshape(2 * own_rows, own_pts)
                prod = jnp.dot(left, block, preferred_element_type=jnp.float32)
                total = prod if total is None else total + prod
            m_re = total[:own_rows, :own_shots] - total[own_rows:, own_shots:]
            m_im = total[:own_rows, own_shots:] + total[own_rows:, :own_shots]
            mbuf[b, rows, :own_shots] = m_re.astype(jnp.bfloat16)
            mbuf[b, rows, own_shots:] = m_im.astype(jnp.bfloat16)
            dst = o_ref.at[my_f, rows_of(lax.rem(i, per_rcv), own_rows), :]
            send(o_src(b, i), dst, (group * per_group + b, j), o_send.at[b, j], o_recv.at[my_f])
            p_re = pbuf[b, rows, :own_shots].astype(jnp.float32)
            p_im = pbuf[b, rows, own_shots:].astype(jnp.float32)

            def down(value):
                return jnp.sum(value.reshape(own_rows // 8, 8, own_shots), axis=0)

            acc[b, 0] += down(m_re * p_re + m_im * p_im)
            acc[b, 1] += down(m_re * p_im - m_im * p_re)
            acc[b, 2] += down(m_re * m_re + m_im * m_im)

        each(0, per_group, one)

    turns = [((t + 1) * n_rcv, 0, t) for t in range(per_group)]
    turns += [((t + 1) * n_rcv, 1, t) for t in range(per_group)]
    for _, own, t in sorted(turns):
        p = lax.rem(place + per_group - t, per_group)
        if own:
            compute(group * per_group + p)
        else:
            each(1, n_groups, lambda gg: compute(lax.rem(group + gg, n_groups) * per_group + p))

    def coefficients(n):
        b = lax.rem(n + place, per_group)
        num_re, num_im, power = (
            jnp.sum(acc[b, v], axis=0, keepdims=True) / float(points) for v in range(3)
        )
        power = power + 1e-6
        row = lax.broadcasted_iota(jnp.int32, (8, own_shots), 0)
        fbuf[b] = jnp.where(row < 4, num_re / power, num_im / power)
        for j in range(n_rcv):
            send(fbuf.at[b], filt_ref.at[my_f], (group * per_group + b, j), f_send.at[b, j], f_recv.at[my_f])

    each(0, per_group, coefficients)

    def sent_results(n):
        b, j = lax.div(n, n_rcv), lax.rem(n, n_rcv)
        target = (group * per_group + b, j)
        sent(fbuf.at[b], target, f_send.at[b, j])
        sent(mbuf.at[b, rows_of(j, own_pts), :], target, o_send.at[b, j])

    def result_arrived(n):
        arrived(o_ref.at[n], o_recv.at[n])
        arrived(filt_ref.at[n], f_recv.at[n])

    each(0, n_freq, result_arrived)
    each(0, n_freq * n_groups, sent_d)
    each(0, n_freq, sent_p)
    each(0, per_group * n_rcv, sent_results)


def subtract_kernel(o_ref, filt_ref, s_ref, live_ref, pred_ref, prim_ref):
    shots = s_ref.shape[3]
    keep = live_ref[...].astype(jnp.bfloat16)
    for f in range(o_ref.shape[0]):
        re, im = o_ref[f, :, :shots], o_ref[f, :, shots:]
        pred_ref[0, f] = re
        pred_ref[1, f] = im
        re, im = re.astype(jnp.float32), im.astype(jnp.float32)
        filt_re, filt_im = filt_ref[f, 0:1, :], filt_ref[f, 4:5, :]
        rec_re = (s_ref[0, f] * keep).astype(jnp.float32)
        rec_im = (s_ref[1, f] * keep).astype(jnp.float32)
        prim_ref[0, f] = (rec_re - (filt_re * re - filt_im * im)).astype(jnp.bfloat16)
        prim_ref[1, f] = (rec_im - (filt_re * im + filt_im * re)).astype(jnp.bfloat16)


def shards(n_shot, n_rcv, data_matrix, shot_records, live):
    _, n_freq, own_rows, own_pts = data_matrix.shape
    own_shots = shot_records.shape[3]
    points = own_pts * n_rcv
    per_group = n_freq // n_rcv
    n_groups = n_shot // per_group
    anywhere = pl.BlockSpec(memory_space=pl.ANY)
    dma = pltpu.SemaphoreType.DMA
    multiples, filt = pl.pallas_call(
        functools.partial(exchange_kernel, n_shot, n_rcv),
        out_shape=(
            jax.ShapeDtypeStruct((n_freq, own_pts, 2 * own_shots), jnp.bfloat16),
            jax.ShapeDtypeStruct((n_freq, 8, own_shots), jnp.float32),
        ),
        in_specs=[anywhere] * 3,
        out_specs=(anywhere, anywhere),
        scratch_shapes=[
            pltpu.VMEM((n_rcv, 2, points, own_pts), jnp.bfloat16),
            pltpu.VMEM((per_group, points, 2 * own_shots), jnp.bfloat16),
            pltpu.VMEM((2, n_freq, own_pts, own_shots), jnp.bfloat16),
            pltpu.VMEM((own_pts, own_shots), jnp.int32),
            pltpu.VMEM((n_freq, own_pts, 2 * own_shots), jnp.bfloat16),
            pltpu.VMEM((per_group, points, 2 * own_shots), jnp.bfloat16),
            pltpu.VMEM((per_group, 8, own_shots), jnp.float32),
            pltpu.VMEM((per_group, 3, 8, own_shots), jnp.float32),
            dma((2,)),
            dma((n_groups, n_freq)),
            dma((n_shot, n_rcv)),
            dma((n_freq,)),
            dma((per_group, n_rcv)),
            dma((per_group, n_rcv)),
            dma((n_freq,)),
            dma((per_group, n_rcv)),
            dma((n_freq,)),
        ],
        compiler_params=pltpu.CompilerParams(
            collective_id=0, has_side_effects=True, vmem_limit_bytes=60 * 1024 * 1024
        ),
    )(data_matrix, shot_records, live)
    step = 4
    pair = pl.BlockSpec((2, step, own_pts, own_shots), lambda f: (0, f, 0, 0))
    out = jax.ShapeDtypeStruct((2, n_freq, own_pts, own_shots), jnp.bfloat16)
    return pl.pallas_call(
        subtract_kernel,
        grid=(n_freq // step,),
        out_shape=(out, out),
        in_specs=[
            pl.BlockSpec((step, own_pts, 2 * own_shots), lambda f: (f, 0, 0)),
            pl.BlockSpec((step, 8, own_shots), lambda f: (f, 0, 0)),
            pair,
            pl.BlockSpec((own_pts, own_shots), lambda f: (0, 0)),
        ],
        out_specs=(pair, pair),
        compiler_params=pltpu.CompilerParams(vmem_limit_bytes=24 * 1024 * 1024),
    )(multiples, filt, shot_records, live)


def solution(mesh):
    in_specs = (P(None, None, "shot", "rcv"), P(None, None, "rcv", "shot"), P("rcv", "shot"))
    out_specs = (P(None, None, "rcv", "shot"), P(None, None, "rcv", "shot"))
    body = functools.partial(shards, mesh.shape["shot"], mesh.shape["rcv"])
    return jax.shard_map(body, mesh=mesh, in_specs=in_specs, out_specs=out_specs, check_vma=False)
```
